32 devices in a mesh: dp: 4 (over z), vocab: 8 (over y, x, core).
Axes of the slice: x: 2, y: 2, z: 4, core: 2. Of those that a mesh axis runs over, the one named last changes fastest.
Arguments:
- base_hidden: bfloat16 [96, 8192], P('dp', 'vocab'), may hold values from -16 to 16
- reinforced_hidden: bfloat16 [96, 8192], P('dp', 'vocab'), may hold values from -16 to 16
- trained_hidden: bfloat16 [96, 8192], P('dp', 'vocab'), may hold values from -16 to 16
- frozen_head: bfloat16 [8192, 16384], P(None, ('dp', 'vocab')), may hold values from -1 to 1
- trained_head: bfloat16 [8192, 16384], P(None, ('dp', 'vocab')), may hold values from -1 to 1
- label_tokens: int32 [96], P('dp'), may hold values from 0 to 16383
- generic_map: int32 [16384], replicated, may hold values from 0 to 16383, as said below
- loss_mask: int32 [96], P('dp'), may hold values 0 or 1
Outputs:
- token_loss: float32 [96], P('dp')
- head_grad: bfloat16 [8192, 16384], P(None, ('dp', 'vocab'))
- hidden_grad: bfloat16 [96, 8192], P('dp', 'vocab')
The draws below stay inside these ranges and needn't reach their ends.
Inputs may be any that keep to these rules, and one draw needn't show every extreme that they name: `generic_map`: maps each token to its generic counterpart; many tokens map to themselves.
All inputs are finite; a program needn't handle non-finite values. No bound on the sum of `loss_mask` on one device may be relied on, other than what follows from the above.
Results may differ from the reference program's by a relative error of at most 0.0065.
Values may be sent and summed in bfloat16 or wider, within the bound.
No kernel may reach another device: no remote copies, remote signals or barrier semaphores. Data moves between devices by JAX's collectives and lax.ppermute only.
A program may use at most 128 MiB of HBM per device.

```python
import math
import jax
import jax.numpy as jnp
from jax import lax

D = 8192
TOKENS = 96
VOCAB = 16384


def head_draw(key, marker):
    values = jax.random.normal(jax.random.fold_in(key, marker + 50), (D, VOCAB), jnp.float32)
    return jnp.clip(values, -6.0, 6.0) / math.sqrt(D)


def hidden_draw(key, marker):
    own_key = jax.random.fold_in(key, marker + 10)
    keys = jax.random.split(own_key, 2)
    return jnp.clip(3.0 * jax.random.normal(keys[1], (TOKENS, D), jnp.float32), -15.0, 15.0)


def draw_base_hidden(key, part):
    return hidden_draw(key, 1).astype(jnp.bfloat16)


def draw_reinforced_hidden(key, part):
    return hidden_draw(key, 2).astype(jnp.bfloat16)


def draw_trained_hidden(key, part):
    return hidden_draw(key, 3).astype(jnp.bfloat16)


def draw_frozen_head(key, part):
    return head_draw(key, 1).astype(jnp.bfloat16)


def draw_trained_head(key, part):
    return head_draw(key, 3).astype(jnp.bfloat16)


def draw_generic_map(key, part):
    keys = jax.random.split(jax.random.fold_in(key, 77), 2)
    itself = jnp.arange(VOCAB, dtype=jnp.int32)
    others = jax.random.randint(keys[0], (VOCAB,), 0, VOCAB).astype(jnp.int32)
    remapped = jax.random.randint(keys[1], (VOCAB,), 0, 4) == 0
    return jnp.where(remapped, others, itself)


def plant(values, rng, low, largest):
    extent = values.shape
    spot = [jax.random.randint(jax.random.fold_in(rng, axis), (), 0, extent[axis]) for axis in range(len(extent))]
    values = values.at[tuple(spot)].set(low)
    longest = extent.index(max(extent))
    spot[longest] = (spot[longest] + 1) % extent[longest]
    return values.at[tuple(spot)].set(largest)


def setup_inputs(seed: int = 0) -> dict:
    streams_of = jax.random.split(jax.random.key(seed), 9)
    return {
        "base_hidden": draw_base_hidden(jax.random.fold_in(streams_of[8], 71), 0),
        "reinforced_hidden": draw_reinforced_hidden(jax.random.fold_in(streams_of[8], 71), 0),
        "trained_hidden": draw_trained_hidden(jax.random.fold_in(streams_of[8], 71), 0),
        "frozen_head": draw_frozen_head(jax.random.fold_in(streams_of[8], 71), 0),
        "trained_head": draw_trained_head(jax.random.fold_in(streams_of[8], 71), 0),
        "label_tokens": plant(jax.random.randint(streams_of[5], (TOKENS,), 0, VOCAB), jax.random.fold_in(streams_of[5], 1), 0, VOCAB - 1).astype(jnp.int32),
        "generic_map": draw_generic_map(jax.random.fold_in(streams_of[8], 71), 0),
        "loss_mask": plant((jax.random.randint(streams_of[7], (TOKENS,), 0, 4) < 3).astype(jnp.int32), jax.random.fold_in(streams_of[7], 1), 0, 1),
    }


reinforce_weight = 2.0
anchor_share = 0.3
loss_scale = 16.0


def reference(base_hidden, reinforced_hidden, trained_hidden, frozen_head, trained_head, label_tokens, generic_map, loss_mask):
    base_logits = jnp.dot(base_hidden, frozen_head, preferred_element_type=jnp.float32)
    reinforced_logits = jnp.dot(reinforced_hidden, frozen_head, preferred_element_type=jnp.float32)
    generic = base_logits - reinforce_weight * jnp.maximum(reinforced_logits - base_logits, 0.0)
    trained_logits = jnp.dot(trained_hidden, trained_head, preferred_element_type=jnp.float32)
    generic_peak = jnp.max(generic, axis=1)
    trained_peak = jnp.max(trained_logits, axis=1)
    generic_exps = jnp.exp(generic - generic_peak[:, None])
    trained_exps = jnp.exp(trained_logits - trained_peak[:, None])
    generic_total = jnp.sum(generic_exps, axis=1)
    trained_total = jnp.sum(trained_exps, axis=1)
    cross_term = jnp.sum(generic_exps * trained_logits, axis=1)
    anchor = generic_map[label_tokens].astype(jnp.int32)
    anchor_hit = jnp.arange(VOCAB, dtype=jnp.int32)[None, :] == anchor[:, None]
    picked_logit = jnp.sum(jnp.where(anchor_hit, trained_logits, 0.0), axis=1)
    token_weight = loss_mask.astype(jnp.float32)
    token_loss = token_weight * (trained_peak + jnp.log(trained_total) - (1.0 - anchor_share) * cross_term / generic_total - anchor_share * picked_logit)
    target = (1.0 - anchor_share) * generic_exps / generic_total[:, None] + anchor_share * anchor_hit.astype(jnp.float32)
    logit_grad = (loss_scale * token_weight[:, None] * (trained_exps / trained_total[:, None] - target)).astype(jnp.bfloat16)
    head_grad = lax.dot_general(trained_hidden, logit_grad, (((0,), (0,)), ((), ())), preferred_element_type=jnp.float32).astype(jnp.bfloat16)
    hidden_grad = lax.dot_general(logit_grad, trained_head, (((1,), (1,)), ((), ())), preferred_element_type=jnp.float32).astype(jnp.bfloat16)
    return (token_loss, head_grad, hidden_grad)
```

```python
import functools

import jax
import jax.numpy as jnp
from jax import lax
from jax.experimental import pallas as pl
from jax.experimental.pallas import tpu as pltpu
from jax.sharding import PartitionSpec as P

reinforce_weight = 2.0
anchor_share = 0.3
loss_scale = 16.0


LANES = 128
VMEM = pltpu.VMEM
BF16 = jnp.bfloat16
F32 = jnp.float32


def params(mib):
    return pltpu.CompilerParams(vmem_limit_bytes=mib * 1024 * 1024)


def vmem_specs(n):
    return [pl.BlockSpec(memory_space=VMEM)] * n


def shape(dims, dtype):
    return jax.ShapeDtypeStruct(dims, dtype)


def swap(x, axis, count, bit):
    return lax.ppermute(x, axis, [(i, i ^ bit) for i in range(count)])


def bits_of(c):
    return [1 << k for k in range(c.bit_length()) if (c >> k) & 1]


def stack_rows(parts):
    return jnp.concatenate([p.astype(F32) for p in parts], axis=0).astype(BF16)


def combine(parts):
    peak_g = functools.reduce(jnp.maximum, [p[0] for p in parts])
    peak_t = functools.reduce(jnp.maximum, [p[3] for p in parts])
    sums = [0.0, 0.0, 0.0, 0.0]
    for p in parts:
        fix_g = jnp.exp(p[0] - peak_g)
        fix_t = jnp.exp(p[3] - peak_t)
        terms = (p[1] * fix_g, p[2] * fix_g, p[4] * fix_t, p[5])
        sums = [s + t for s, t in zip(sums, terms)]
    return [peak_g, sums[0], sums[1], peak_t, sums[2], sums[3]]


def place_lanes(cols, rows):
    lane = lax.broadcasted_iota(jnp.int32, (rows, LANES), 1)
    out = jnp.zeros((rows, LANES), F32)
    for k, col in enumerate(cols):
        out = jnp.where(lane == k, col, out)
    return out


def pack_kernel(tl, a, b, c, o, sem):
    copies = [
        pltpu.make_async_copy(src, o.at[pl.ds(k * tl, tl), :], sem.at[k])
        for k, src in enumerate((a, b, c))
    ]
    for cp in copies:
        cp.start()
    for cp in copies:
        cp.wait()


def logits_kernel(offset, dp, tl, feat, first, last, *refs):
    refs = list(refs)
    own = [refs.pop(0) for _ in range(dp)]
    sib = refs.pop(0)
    wf, wt = refs.pop(0), refs.pop(0)
    acc_in = None if first else (refs.pop(0), refs.pop(0))
    tags = refs.pop(0) if last else None
    out_f, out_t, rows_out = refs.pop(0), refs.pop(0), refs.pop(0)
    stats = refs.pop(0) if last else None
    buf_f, buf_t, sem = refs
    v = lax.axis_index("vocab")
    copies = []
    for k in range(2):
        row = pl.multiple_of((v ^ (offset ^ k)) * feat, feat)
        pair = (
            pltpu.make_async_copy(wf.at[pl.ds(row, feat), :], buf_f.at[k], sem.at[k, 0]),
            pltpu.make_async_copy(wt.at[pl.ds(row, feat), :], buf_t.at[k], sem.at[k, 1]),
        )
        for cp in pair:
            cp.start()
        copies.append(pair)
    acc_f = acc_t = None
    for k in range(2):
        if k == 0:
            frozen = [r[0 : 2 * tl, :] for r in own]
            trained = [r[2 * tl : 3 * tl, :] for r in own]
        else:
            frozen = [sib[3 * tl * j : 3 * tl * j + 2 * tl, :] for j in range(dp)]
            trained = [sib[3 * tl * j + 2 * tl : 3 * tl * (j + 1), :] for j in range(dp)]
        fr = jnp.concatenate(frozen, axis=0)
        tr = stack_rows(trained)
        rows_out[k] = tr
        copies[k][0].wait()
        part_f = jnp.dot(fr, buf_f[k], preferred_element_type=F32)
        copies[k][1].wait()
        part_t = jnp.dot(tr, buf_t[k], preferred_element_type=F32)
        acc_f = part_f if acc_f is None else acc_f + part_f
        acc_t = part_t if acc_t is None else acc_t + part_t
    if not first:
        acc_f = acc_f + acc_in[0][...]
        acc_t = acc_t + acc_in[1][...]
    if not last:
        out_f[...] = acc_f
        out_t[...] = acc_t
        return
    base = jnp.concatenate([acc_f[2 * tl * j : 2 * tl * j + tl] for j in range(dp)], axis=0)
    reinf = jnp.concatenate([acc_f[2 * tl * j + tl : 2 * tl * (j + 1)] for j in range(dp)], axis=0)
    generic = base - reinforce_weight * jnp.maximum(reinf - base, 0.0)
    out_f[...] = generic
    out_t[...] = acc_t
    tokens, width = generic.shape
    start = (lax.axis_index("dp") * lax.axis_size("vocab") + v) * width
    column = lax.broadcasted_iota(jnp.int32, (tokens, width), 1) + start
    hit = column == tags[:, 0:1].astype(jnp.int32)
    peak_g = jnp.max(generic, axis=1, keepdims=True)
    peak_t = jnp.max(acc_t, axis=1, keepdims=True)
    exps_g = jnp.exp(generic - peak_g)
    cols = [
        peak_g,
        jnp.sum(exps_g, axis=1, keepdims=True),
        jnp.sum(exps_g * acc_t, axis=1, keepdims=True),
        peak_t,
        jnp.sum(jnp.exp(acc_t - peak_t), axis=1, keepdims=True),
        jnp.sum(jnp.where(hit, acc_t, 0.0), axis=1, keepdims=True),
    ]
    table = place_lanes(cols, tokens)
    padded = stats.shape[1]
    if padded > tokens:
        table = jnp.concatenate([table, jnp.zeros((padded - tokens, LANES), F32)], axis=0)
    stats[...] = jnp.transpose(table)[0:8, :]


def merge_kernel(*refs):
    out = refs[-1]
    parts = [[r[k : k + 1, :] for k in range(6)] for r in refs[:-1]]
    got = combine(parts)
    out[...] = jnp.concatenate(got + [jnp.zeros((2, out.shape[1]), F32)], axis=0)


def grad_kernel(dp, tl, feat, chunks, generic, trained, tags, wt, *refs):
    stats, (grad, loss, out, buf, sem) = refs[:dp], refs[dp:]
    v = lax.axis_index("vocab")
    copies = []
    for k, c in enumerate(chunks):
        row = pl.multiple_of((v ^ c) * feat, feat)
        copies.append(pltpu.make_async_copy(wt.at[pl.ds(row, feat), :], buf.at[k], sem.at[k]))
        copies[-1].start()
    tokens, width = generic.shape
    parts = []
    for b in range(dp):
        tile = stats[b][...]
        full = jnp.concatenate([tile, jnp.zeros((LANES - 8, tile.shape[1]), F32)], axis=0)
        table = jnp.transpose(full)
        if b:
            table = jnp.concatenate(
                [table[tl * (j ^ b) : tl * ((j ^ b) + 1)] for j in range(dp)], axis=0
            )
        parts.append([table[:tokens, k : k + 1] for k in range(6)])
    peak_g, total_g, cross, peak_t, total_t, picked = combine(parts)
    weight = tags[:, 1:2]
    value = weight * (
        peak_t
        + jnp.log(total_t)
        - (1.0 - anchor_share) * cross / total_g
        - anchor_share * picked
    )
    loss[...] = jnp.broadcast_to(value, loss.shape)
    start = (lax.axis_index("dp") * lax.axis_size("vocab") + v) * width
    column = lax.broadcasted_iota(jnp.int32, (tokens, width), 1) + start
    hit = (column == tags[:, 0:1].astype(jnp.int32)).astype(F32)
    exps_g = jnp.exp(generic[...] - peak_g)
    exps_t = jnp.exp(trained[...] - peak_t)
    target = (1.0 - anchor_share) * exps_g / total_g + anchor_share * hit
    lg = (loss_scale * weight * (exps_t / total_t - target)).astype(BF16)
    grad[...] = lg
    for k in range(len(chunks)):
        copies[k].wait()
        part = lax.dot_general(
            lg, buf[k], (((1,), (1,)), ((), ())), preferred_element_type=F32
        )
        out[pl.ds(k * tokens, tokens), :] = part.astype(BF16)


def own_kernel(feat, chunks, lg, wt, out, buf, sem):
    v = lax.axis_index("vocab")
    copies = []
    for k, c in enumerate(chunks):
        row = pl.multiple_of((v ^ c) * feat, feat)
        copies.append(pltpu.make_async_copy(wt.at[pl.ds(row, feat), :], buf.at[k], sem.at[k]))
        copies[-1].start()
    for k in range(len(chunks)):
        copies[k].wait()
        out[k] = lax.dot_general(
            lg[...], buf[k], (((1,), (1,)), ((), ())), preferred_element_type=F32
        )


def fold_kernel(tokens, own, got, keep, *outs):
    for k in range(own.shape[0]):
        total = own[k] + got[pl.ds(k * tokens, tokens), :].astype(F32)
        if k == 0:
            keep[...] = total
        else:
            outs[k - 1][...] = total.astype(BF16)


def plane_kernel(tl, count, *refs):
    keep, got, (mine, *outs) = refs[0], refs[1 : 1 + count], refs[1 + count :]
    total = keep[...]
    for r in got:
        total = total + r[...].astype(F32)
    mine[...] = total[0:tl]
    for b, o in enumerate(outs):
        o[...] = total[(b + 1) * tl : (b + 2) * tl].astype(BF16)


def final_kernel(mine, *refs):
    total = mine[...]
    for r in refs[:-1]:
        total = total + r[...].astype(F32)
    refs[-1][...] = total.astype(BF16)


def head_kernel(feat, order, *refs):
    count = len(order)
    lg, rows = refs[0], refs[1 : 1 + count]
    out, buf, sem = refs[1 + count :]
    v = lax.axis_index("vocab")
    copies = []
    step = 0
    for rref, offset in zip(rows, order):
        for k in range(2):
            slot = step % 2
            if step >= 2:
                copies[step - 2].wait()
            buf[slot] = lax.dot_general(
                rref[k], lg[...], (((0,), (0,)), ((), ())), preferred_element_type=F32
            ).astype(BF16)
            row = pl.multiple_of((v ^ (offset ^ k)) * feat, feat)
            copies.append(
                pltpu.make_async_copy(buf.at[slot], out.at[pl.ds(row, feat), :], sem.at[slot])
            )
            copies[-1].start()
            step += 1
    for cp in copies[-2:]:
        cp.wait()


def on_device(
    base_hidden,
    reinforced_hidden,
    trained_hidden,
    frozen_head,
    trained_head,
    label_tokens,
    generic_map,
    loss_mask,
):
    tl, feat = base_hidden.shape
    dp = lax.axis_size("dp")
    vc = lax.axis_size("vocab")
    tokens = dp * tl
    width = trained_head.shape[1]
    chips = list(range(0, vc, 2))
    padded = -(-tokens // LANES) * LANES
    hbm = pl.BlockSpec(memory_space=pl.ANY)
    dma = pltpu.SemaphoreType.DMA

    packed = pl.pallas_call(
        functools.partial(pack_kernel, tl),
        out_shape=shape((3 * tl, feat), BF16),
        in_specs=[hbm] * 3,
        out_specs=pl.BlockSpec(memory_space=VMEM),
        scratch_shapes=[dma((3,))],
        compiler_params=params(4),
    )(base_hidden, reinforced_hidden, trained_hidden)

    blocks = {0: [packed] + [swap(packed, "dp", dp, b) for b in range(1, dp)]}
    for c in sorted(chips[1:], key=lambda c: len(bits_of(c))):
        bits = bits_of(c)
        blocks[c] = []
        for b in range(dp):
            bit = bits[b % len(bits)]
            blocks[c].append(swap(blocks[c ^ bit][b], "vocab", vc, bit))

    anchor = generic_map[label_tokens]
    tag = jnp.stack([anchor.astype(F32), loss_mask.astype(F32)])
    tag_all = jnp.concatenate([tag] + [swap(tag, "dp", dp, b) for b in range(1, dp)], axis=1)
    tags = jnp.pad(tag_all.T, ((0, 0), (0, LANES - 2)))

    order = sorted(chips, key=lambda c: len(bits_of(c)))
    acc = None
    rows_of = {}
    for n, c in enumerate(order):
        first, last = n == 0, n == len(order) - 1
        sib = swap(jnp.concatenate(blocks[c], axis=0), "vocab", vc, 1)
        ins = [*blocks[c], sib, frozen_head, trained_head]
        specs = vmem_specs(dp + 1) + [hbm, hbm]
        aliases = {}
        if not first:
            ins += acc
            specs += vmem_specs(2)
        if last:
            ins.append(tags)
            specs += vmem_specs(1)
        outs = [
            shape((tokens if last else 2 * tokens, width), F32),
            shape((tokens, width), F32),
            shape((2, tokens, feat), BF16),
        ]
        if last:
            outs.append(shape((8, padded), F32))
        got = pl.pallas_call(
            functools.partial(logits_kernel, c, dp, tl, feat, first, last),
            out_shape=outs,
            in_specs=specs,
            out_specs=vmem_specs(len(outs)),
            scratch_shapes=[
                VMEM((2, feat, width), BF16),
                VMEM((2, feat, width), BF16),
                dma((2, 2)),
            ],
            compiler_params=params(24),
            cost_estimate=pl.CostEstimate(
                flops=12 * tokens * feat * width,
                bytes_accessed=8 * feat * width,
                transcendentals=0,
            ),
            name=f"logits_{n}",
        )(*ins)
        acc, rows_of[c] = [got[0], got[1]], got[2]
    generic, trained = acc
    tile = got[3]

    def merge(tiles):
        return pl.pallas_call(
            merge_kernel,
            out_shape=shape((8, padded), F32),
            in_specs=vmem_specs(len(tiles)),
            out_specs=pl.BlockSpec(memory_space=VMEM),
            compiler_params=params(4),
            name="merge",
        )(*tiles)

    tile = merge([tile, swap(tile, "vocab", vc, 1)])
    tile = merge([tile] + [swap(tile, "vocab", vc, c) for c in chips[1:]])
    tiles = [tile] + [swap(tile, "dp", dp, b) for b in range(1, dp)]

    half = len(chips)
    lg, loss, away = pl.pallas_call(
        functools.partial(grad_kernel, dp, tl, feat, [c ^ 1 for c in chips]),
        out_shape=[
            shape((tokens, width), BF16),
            shape((tokens, LANES), F32),
            shape((half * tokens, feat), BF16),
        ],
        in_specs=vmem_specs(3) + [hbm] + vmem_specs(dp),
        out_specs=vmem_specs(3),
        scratch_shapes=[VMEM((half, feat, width), BF16), dma((half,))],
        compiler_params=params(24),
        name="grad",
    )(generic, trained, tags, trained_head, *tiles)
    got = swap(away, "vocab", vc, 1)
    own = pl.pallas_call(
        functools.partial(own_kernel, feat, chips),
        out_shape=shape((half, tokens, feat), F32),
        in_specs=vmem_specs(1) + [hbm],
        out_specs=pl.BlockSpec(memory_space=VMEM),
        scratch_shapes=[VMEM((half, feat, width), BF16), dma((half,))],
        compiler_params=params(24),
        cost_estimate=pl.CostEstimate(
            flops=2 * half * tokens * feat * width,
            bytes_accessed=2 * half * feat * width,
            transcendentals=0,
        ),
        name="own",
    )(lg, trained_head)
    folded = pl.pallas_call(
        functools.partial(fold_kernel, tokens),
        out_shape=[shape((tokens, feat), F32)] + [shape((tokens, feat), BF16)] * (half - 1),
        in_specs=vmem_specs(2),
        out_specs=vmem_specs(half),
        compiler_params=params(16),
        name="fold",
    )(own, got)
    sent = [swap(p, "vocab", vc, c) for p, c in zip(folded[1:], chips[1:])]
    head_grad = pl.pallas_call(
        functools.partial(head_kernel, feat, order),
        out_shape=shape((vc * feat, width), BF16),
        in_specs=vmem_specs(1 + len(order)),
        out_specs=hbm,
        scratch_shapes=[VMEM((2, feat, width), BF16), dma((2,))],
        compiler_params=params(24),
        cost_estimate=pl.CostEstimate(
            flops=2 * vc * tokens * feat * width,
            bytes_accessed=2 * vc * feat * width,
            transcendentals=0,
        ),
        name="head",
    )(lg, *[rows_of[c] for c in order])
    plane = pl.pallas_call(
        functools.partial(plane_kernel, tl, len(sent)),
        out_shape=[shape((tl, feat), F32)] + [shape((tl, feat), BF16)] * (dp - 1),
        in_specs=vmem_specs(1 + len(sent)),
        out_specs=vmem_specs(dp),
        compiler_params=params(16),
        name="plane",
    )(folded[0], *sent)
    back = [swap(p, "dp", dp, b + 1) for b, p in enumerate(plane[1:])]
    hidden_grad = pl.pallas_call(
        final_kernel,
        out_shape=shape((tl, feat), BF16),
        in_specs=vmem_specs(dp),
        out_specs=pl.BlockSpec(memory_space=VMEM),
        compiler_params=params(4),
        name="final",
    )(plane[0], *back)
    token_loss = loss[:tl, 0]
    return token_loss, head_grad, hidden_grad


def solution(mesh):
    placed = (
        P("dp", "vocab"),
        P("dp", "vocab"),
        P("dp", "vocab"),
        P(None, ("dp", "vocab")),
        P(None, ("dp", "vocab")),
        P("dp"),
        P(),
        P("dp"),
    )
    return jax.shard_map(
        on_device,
        mesh=mesh,
        in_specs=placed,
        out_specs=(P("dp"), P(None, ("dp", "vocab")), P("dp", "vocab")),
        check_vma=False,
    )
```
